32 devices in a mesh: grp: 4 (over z), dom: 8 (over y, x, core).
Axes of the slice: x: 2, y: 2, z: 4, core: 2. Of those that a mesh axis runs over, the one named last changes fastest.
Arguments:
- local_inverse: bfloat16 [160, 640, 640], P(('grp', 'dom')), may hold values from -0.25 to 0.25
- local_trace: bfloat16 [160, 640, 480], P(('grp', 'dom')), may hold values from -0.25 to 0.25
- trace_local: bfloat16 [160, 480, 640], P(('grp', 'dom')), may hold values from -0.25 to 0.25
- trace_trace: bfloat16 [160, 480, 480], P(('grp', 'dom')), may hold values from -0.25 to 0.25
- local_rhs: bfloat16 [160, 640], P(('grp', 'dom')), may hold values from -6 to 6
- trace_rhs: bfloat16 [160, 480], P(('grp', 'dom')), may hold values from -6 to 6
- trace_state: bfloat16 [480, 80], P(('grp', 'dom')), may hold values from -6 to 6
- side_owner: int32 [160, 6], P(('grp', 'dom')), may hold values from 0 to 31, as said below
- side_slot: int32 [160, 6], P(('grp', 'dom')), may hold values from 0 to 3, as said below
- face_slots: int32 [480, 2], P(('grp', 'dom')), may hold values from 0 to 31, as said below
Outputs:
- residual: float32 [480, 80], P(('grp', 'dom'))
- image: float32 [480, 80], P(('grp', 'dom'))
The draws below stay inside these ranges and needn't reach their ends.
Inputs may be any that keep to these rules, and one draw needn't show every extreme that they name: `side_owner`: an element on the device with grp index g and dom index d has every side owned by a device of grp index g or (g + 1) mod 4; exactly 15 of one device's sides have their owner in each of the two rows. `side_slot`: Take, at grp index g and dom index d, the sides of that device's elements owned in row g together with the sides of the device at grp index (g - 1) mod 4 and the same dom index owned in row g: among those with their owner at one dom index, the slots are distinct. Every element side's receive position is named by exactly one entry of face_slots at its owner, and every entry names one side; each face has two sides of different elements.
All inputs are finite; a program needn't handle non-finite values.
Results may differ from the reference program's by a relative error of at most 0.0065.
Values may be sent and summed in bfloat16 or wider, within the bound.
A program may use at most 64 MiB of HBM per device.

```python
import jax
import jax.numpy as jnp
from jax import lax

NL = 640
FD = 80
NT = 480
E_DEV = 5
F_DEV = 15
CAP = 4
ELEMS = 160
FACES = 480
N_GRP = 4
N_DOM = 8
DEVICES = 32


def build_routes(key):
    half = CAP // 2
    first, second, third = jax.random.split(jax.random.fold_in(key, 7), 3)
    ranking = jax.random.permutation(first, N_DOM).astype(jnp.int32)
    dom_values = jnp.arange(N_DOM, dtype=jnp.int32)
    scores = jnp.where(dom_values == 1, -3, jnp.where(dom_values == N_DOM - 1, -2, jnp.where(dom_values == N_DOM // 2, -1, ranking))).astype(jnp.int32)
    dom_order = jnp.argsort(scores, stable=True).astype(jnp.int32)
    index_face = jnp.arange(F_DEV, dtype=jnp.int32)
    offsets = dom_order[index_face % N_DOM]
    repeat_rank = index_face // N_DOM
    face_order = jax.random.permutation(second, F_DEV).astype(jnp.int32)
    devices_ids = jnp.arange(DEVICES, dtype=jnp.int32)
    grp_ids = devices_ids // N_DOM
    dom_ids = devices_ids % N_DOM
    side_order = jax.vmap(lambda sub: jax.random.permutation(sub, 2 * F_DEV))(jax.random.split(third, DEVICES)).astype(jnp.int32)
    kinds = jnp.arange(2 * F_DEV, dtype=jnp.int32)
    kind_face = kinds % F_DEV
    upper = (kinds >= F_DEV).astype(jnp.int32)
    owner_grp = (grp_ids[:, None] + upper[None, :]) % N_GRP
    owner_dom = (dom_ids[:, None] + offsets[kind_face][None, :]) % N_DOM
    owner = owner_grp * N_DOM + owner_dom
    slot = jnp.broadcast_to(repeat_rank[kind_face] + half * upper, (DEVICES, 2 * F_DEV))
    rows = jnp.broadcast_to(devices_ids[:, None], (DEVICES, 2 * F_DEV))
    owner_sides = jnp.zeros((DEVICES, 2 * F_DEV), jnp.int32).at[rows, side_order].set(owner)
    slot_sides = jnp.zeros((DEVICES, 2 * F_DEV), jnp.int32).at[rows, side_order].set(slot)
    next_face = (index_face + 1) % F_DEV
    lower_pos = (dom_ids[:, None] - offsets[None, :]) % N_DOM * CAP + repeat_rank[None, :]
    upper_pos = (dom_ids[:, None] - offsets[next_face][None, :]) % N_DOM * CAP + half + repeat_rank[next_face][None, :]
    pairs = jnp.stack([lower_pos, upper_pos], axis=2)
    face_table = jnp.zeros((DEVICES, F_DEV, 2), jnp.int32).at[:, face_order, :].set(pairs)
    return (owner_sides.reshape(DEVICES * E_DEV, 6), slot_sides.reshape(DEVICES * E_DEV, 6), face_table.reshape(DEVICES * F_DEV, 2))


def draw_side_owner(key, part):
    return build_routes(key)[0]


def draw_side_slot(key, part):
    return build_routes(key)[1]


def draw_face_slots(key, part):
    return build_routes(key)[2]


def shard_levels(rng, extent, cuts, low, high):
    level = 1.0
    for position, blocks in cuts:
        draws = jax.random.uniform(jax.random.fold_in(jax.random.fold_in(rng, 6), position), (blocks,), jnp.float32, low / len(cuts), high / len(cuts))
        level = level * jnp.repeat(jnp.exp(draws), extent[position] // blocks).reshape((-1,) + (1,) * (len(extent) - 1 - position))
    return level


def centred(own_key, shape, spread, bound, cuts=(), kind=jnp.bfloat16):
    entries = spread * jax.random.normal(own_key, shape, jnp.float32)
    if cuts:
        entries = entries * shard_levels(own_key, shape, cuts, -0.22, 0.18)
    return jnp.clip(entries, -bound, bound).astype(kind)


def setup_inputs(seed: int = 0) -> dict:
    keys = jax.random.split(jax.random.key(seed), 11)
    local_inverse = centred(keys[0], (ELEMS, NL, NL), NL ** -0.5, 0.25, ((0, 32),))
    local_trace = centred(keys[1], (ELEMS, NL, NT), NT ** -0.5, 0.25, ((0, 32),))
    trace_local = centred(keys[2], (ELEMS, NT, NL), NL ** -0.5, 0.25, ((0, 32),))
    trace_trace = centred(keys[3], (ELEMS, NT, NT), NT ** -0.5, 0.25, ((0, 32),))
    local_rhs = centred(keys[4], (ELEMS, NL), 1.0, 6.0, ((0, 32),))
    trace_rhs = centred(keys[5], (ELEMS, NT), 1.0, 6.0, ((0, 32),))
    trace_state = centred(keys[6], (FACES, FD), 1.0, 6.0, ((0, 32),))
    side_owner = draw_side_owner(jax.random.fold_in(keys[10], 71), 0)
    side_slot = draw_side_slot(jax.random.fold_in(keys[10], 71), 0)
    face_slots = draw_face_slots(jax.random.fold_in(keys[10], 71), 0)
    return {"local_inverse": local_inverse, "local_trace": local_trace, "trace_local": trace_local, "trace_trace": trace_trace, "local_rhs": local_rhs, "trace_rhs": trace_rhs, "trace_state": trace_state, "side_owner": side_owner, "side_slot": side_slot, "face_slots": face_slots}


def condense(block):
    inverse, coupling, back, diagonal, interior, boundary = block
    coupled = jnp.einsum('eij,ejk->eik', inverse.astype(jnp.float32), coupling.astype(jnp.float32)).astype(jnp.bfloat16)
    coupled = lax.optimization_barrier(coupled)
    solved = jnp.einsum('eij,ej->ei', inverse.astype(jnp.float32), interior.astype(jnp.float32)).astype(jnp.bfloat16)
    solved = lax.optimization_barrier(solved)
    schur = diagonal.astype(jnp.float32) - jnp.einsum('eij,ejk->eik', back.astype(jnp.float32), coupled.astype(jnp.float32))
    condensed = boundary.astype(jnp.float32) - jnp.einsum('eij,ej->ei', back.astype(jnp.float32), solved.astype(jnp.float32))
    return schur.astype(jnp.bfloat16), condensed.astype(jnp.bfloat16)


def reference(local_inverse, local_trace, trace_local, trace_trace, local_rhs, trace_rhs, trace_state, side_owner, side_slot, face_slots):
    positions = N_DOM * CAP
    elements = E_DEV * DEVICES
    arrays = (local_inverse, local_trace, trace_local, trace_trace, local_rhs, trace_rhs)
    blocks = tuple(item.reshape((DEVICES, E_DEV) + item.shape[1:]) for item in arrays)
    schur, condensed = lax.map(condense, blocks)
    condensed = condensed.reshape(elements, NT)
    element_ids = jnp.arange(elements).astype(jnp.int32)
    holder_dom = (element_ids // E_DEV) % N_DOM
    receive = (side_owner * positions + holder_dom[:, None] * CAP + side_slot).reshape(-1).astype(jnp.int32)
    face_owner = (jnp.arange(FACES).astype(jnp.int32) // F_DEV).astype(jnp.int32)
    face_pos = (face_owner[:, None] * positions + face_slots).astype(jnp.int32)
    face_ids = jnp.repeat(jnp.arange(FACES).astype(jnp.int32), 2)
    pos_face = jnp.zeros((DEVICES * positions,), jnp.int32).at[face_pos.reshape(-1)].set(face_ids)
    side_face = pos_face[receive]

    def apply(vector):
        gathered = vector[side_face].reshape(DEVICES, E_DEV, NT)

        def one(pair):
            blocks_dev, values = pair
            return jnp.einsum('ekj,ej->ek', blocks_dev.astype(jnp.float32), values.astype(jnp.float32))

        return lax.map(one, (schur, gathered)).reshape(elements, NT)

    def assemble(terms):
        arrived = jnp.zeros((DEVICES * positions, FD), jnp.float32).at[receive].add(terms.reshape(-1, FD))
        return arrived[face_pos[:, 0]] + arrived[face_pos[:, 1]]

    residual = assemble(apply(trace_state) - condensed.astype(jnp.float32))
    direction = residual.astype(jnp.bfloat16)
    image = assemble(apply(direction))
    return residual, image
```

```python
import functools

import jax
import jax.numpy as jnp
from jax import lax
from jax.experimental import pallas as pl
from jax.experimental.pallas import tpu as pltpu
from jax.sharding import PartitionSpec as P

F32 = jnp.float32
BF16 = jnp.bfloat16
LANES = 128
ROWS = 8
LINK = jnp.bfloat16
MESH = pl.DeviceIdType.MESH


def iota(shape, axis):
    return lax.broadcasted_iota(jnp.int32, shape, axis)


def dot_nn(a, b):
    return jnp.dot(a, b, preferred_element_type=F32)


def dot_nt(a, b):
    return lax.dot_general(a, b, (((1,), (1,)), ((), ())), preferred_element_type=F32)


def kernel(
    grps,
    doms,
    inv_hbm,
    lt_hbm,
    tl_hbm,
    tt_hbm,
    lrhs_hbm,
    trhs_hbm,
    state_hbm,
    owner_hbm,
    slot_hbm,
    face_hbm,
    out_ref,
    lrhs_ref,
    trhs_ref,
    state_ref,
    owner_ref,
    slot_ref,
    face_ref,
    inv_v,
    lt_v,
    tl_v,
    tt_v,
    schur_v,
    state_v,
    down_src,
    down_dst,
    term_src,
    term_dst,
    load_sem,
    small_sem,
    down_send,
    down_recv,
    term_send,
    term_recv,
):
    g = lax.axis_index("grp")
    d = lax.axis_index("dom")
    elements = inv_hbm.shape[0]
    width = tt_hbm.shape[1]
    faces = face_ref.shape[1]
    fd = state_ref.shape[1]
    per_elem = owner_ref.shape[1]
    cap = 2 * ((faces + doms - 1) // doms)
    span = doms * cap
    positions = doms * ROWS
    table = 2 * positions
    face_rows = state_v.shape[0]
    wide = (width // LANES + 1) * LANES
    up_g = lax.rem(g + 1, grps)
    dn_g = lax.rem(g + grps - 1, grps)

    def loads(e):
        pairs = (
            (inv_hbm, inv_v.at[e]),
            (lt_hbm, lt_v.at[e, pl.ds(0, width)]),
            (tl_hbm, tl_v.at[e]),
            (tt_hbm, tt_v.at[e]),
        )
        return [
            pltpu.make_async_copy(src.at[e], dst, load_sem.at[e, i])
            for i, (src, dst) in enumerate(pairs)
        ]

    smalls = [
        pltpu.make_async_copy(src, dst, small_sem.at[i])
        for i, (src, dst) in enumerate(
            (
                (owner_hbm, owner_ref),
                (slot_hbm, slot_ref),
                (face_hbm, face_ref),
                (state_hbm, state_ref),
                (lrhs_hbm, lrhs_ref),
                (trhs_hbm, trhs_ref),
            )
        )
    ]
    for copy in smalls:
        copy.start()

    barrier = pltpu.get_barrier_semaphore()
    for j in range(doms):
        peer = lax.rem(d + j, doms)
        for row in (up_g, dn_g) if j == 0 else (g, up_g, dn_g):
            pl.semaphore_signal(barrier, inc=1, device_id=(row, peer), device_id_type=MESH)

    for e in range(elements):
        for copy in loads(e):
            copy.start()

    for copy in smalls:
        copy.wait()

    def padded(pos):
        return pos // cap * ROWS + lax.rem(pos, cap)

    raw = [[face_ref[i, f] for f in range(faces)] for i in range(2)]
    lane8 = iota((ROWS, LANES), 1)
    row1 = iota((ROWS, 1), 0)
    face_iota = iota((face_rows, 1), 0)
    pos_iota = iota((positions, LANES), 0)
    hits, face_cols = [], []
    for i in range(2):
        row = jnp.full((ROWS, LANES), -1, jnp.int32)
        col = jnp.full((face_rows, 1), -1, jnp.int32)
        for f in range(faces):
            row = jnp.where(lane8 == f, padded(raw[i][f]), row)
            col = jnp.where(face_iota == f, raw[i][f], col)
        hits.append(jnp.where(pos_iota == row[0:1, :], 1.0, 0.0).astype(BF16)[:, :face_rows])
        face_cols.append(col)

    srow = jnp.full((ROWS, LANES), -1, jnp.int32)
    fetch_cols, base_cols, dom_cols, pos_cols = [], [], [], []
    low = jnp.int32(0)
    high = jnp.int32(0)
    for k in range(per_elem):
        fetch_col = jnp.full((ROWS, 1), -1, jnp.int32)
        base_col = jnp.full((ROWS, 1), -4 * doms * span, jnp.int32)
        dom_col = jnp.zeros((ROWS, 1), jnp.int32)
        pos_col = jnp.zeros((ROWS, 1), jnp.int32)
        for e in range(elements):
            owner = owner_ref[e, k]
            own_g = owner // doms
            own_d = owner - own_g * doms
            slot = slot_ref[e, k]
            lift = jnp.where(own_g == g, 0, 1)
            hit = row1 == e
            fetch_col = jnp.where(hit, lift * positions + own_d * ROWS + slot, fetch_col)
            base_col = jnp.where(hit, (2 * lift * doms + own_d) * span + 1, base_col)
            dom_col = jnp.where(hit, own_d, dom_col)
            pos_col = jnp.where(hit, d * cap + slot + 1, pos_col)
            place = jnp.where(own_g == g, low, face_rows + high)
            srow = jnp.where(lane8 == k * ROWS + e, place, srow)
            high = high + lift
            low = low + 1 - lift
        fetch_cols.append(fetch_col)
        base_cols.append(base_col)
        dom_cols.append(dom_col)
        pos_cols.append(pos_col)
    side_rows = per_elem * ROWS
    fetch_hot = jnp.where(
        iota((side_rows, table), 1) == jnp.concatenate(fetch_cols, axis=0), 1.0, 0.0
    ).astype(BF16)
    place_hot = jnp.where(iota((2 * face_rows, LANES), 0) == srow[0:1, :], 1.0, 0.0).astype(BF16)[
        :, :side_rows
    ]
    base = jnp.concatenate(base_cols, axis=0).astype(F32)
    lane_s = iota((side_rows, LANES), 1)
    stamp = jnp.where(
        lane_s == fd,
        jnp.concatenate(dom_cols, axis=0).astype(F32),
        jnp.where(lane_s == fd + 1, jnp.concatenate(pos_cols, axis=0).astype(F32), 0.0),
    ).astype(BF16)

    state_v[...] = jnp.zeros_like(state_v)
    state_v[0:faces, 0:fd] = state_ref[...].astype(F32)
    spare = wide - width
    rhs = lrhs_ref[...].astype(F32)
    spare_row = iota((spare, rhs.shape[1]), 0)
    for e in range(elements):
        lt_v[e, width:wide, :] = jnp.where(spare_row == 0, rhs[e : e + 1, :], 0.0).astype(BF16)

    def down_copies(incoming=False):
        copies = []
        for j in range(doms):
            peer = lax.rem(d + j, doms)
            for lift, row in ((0, g), (1, dn_g)):
                if j == 0 and lift == 0:
                    continue
                copies.append(
                    pltpu.make_async_remote_copy(
                        src_ref=down_src.at[peer],
                        dst_ref=down_dst.at[lift, peer if incoming else d],
                        send_sem=down_send.at[lift, peer],
                        recv_sem=down_recv.at[lift, peer if incoming else d],
                        device_id=(row, peer),
                        device_id_type=MESH,
                    )
                )
        return copies

    regions = ((0, g), (1, up_g), (0, dn_g), (1, g))

    def term_copies(turn, incoming=False):
        copies = []
        for j in range(doms):
            peer = lax.rem(d + j, doms)
            for r in range(4 - 2 * turn):
                half, row = regions[r]
                if j == 0 and r in (0, 3):
                    continue
                copies.append(
                    pltpu.make_async_remote_copy(
                        src_ref=term_src.at[turn, half],
                        dst_ref=term_dst.at[turn, r, peer if incoming else d],
                        send_sem=term_send.at[turn, r, peer],
                        recv_sem=term_recv.at[turn, r, peer if incoming else d],
                        device_id=(row, peer),
                        device_id_type=MESH,
                    )
                )
        return copies

    def send_state():
        lane_f = iota((face_rows, LANES), 1)
        rows = dot_nn(hits[0] + hits[1], state_v[...].astype(BF16))
        for i in range(2):
            other = jnp.where(lane_f == fd, face_cols[1 - i].astype(F32), 0.0).astype(BF16)
            rows = rows + dot_nn(hits[i], other)
        down_src[...] = rows.reshape(doms, ROWS, LANES).astype(LINK)
        for copy in down_copies():
            copy.start()
        down_dst[0, d] = down_src[d]

    def spread_faces(sides):
        total = jnp.zeros((ROWS, wide), F32)
        for k in range(per_elem):
            piece = jnp.concatenate(
                [sides[k * ROWS : (k + 1) * ROWS, :], jnp.zeros((ROWS, wide - LANES), F32)], axis=1
            )
            total = total + (piece if k == 0 else pltpu.roll(piece, k * fd, 1))
        return total

    row_wide = iota((ROWS, width), 0)

    def apply(vector):
        total = jnp.zeros((ROWS, width), F32)
        for e in range(elements):
            total = total + jnp.where(row_wide == e, dot_nt(vector.astype(BF16), schur_v[e]), 0.0)
        return total

    lane_fd = iota((ROWS, LANES), 1) < fd

    def send_terms(turn, terms):
        full = jnp.concatenate([terms, jnp.zeros((ROWS, wide - width), F32)], axis=1)
        pieces = []
        for k in range(per_elem):
            moved = full if k == 0 else pltpu.roll(full, wide - k * fd, 1)
            pieces.append(jnp.where(lane_fd, moved[:, :LANES], 0.0))
        sides = jnp.concatenate(pieces, axis=0).astype(BF16)
        rows = dot_nn(place_hot, sides + stamp)
        term_src[turn] = rows.reshape(2, face_rows, LANES).astype(BF16)
        for copy in term_copies(turn):
            copy.start()
        term_dst[turn, 0, d] = term_src[turn, 0]
        if turn == 0:
            term_dst[turn, 3, d] = term_src[turn, 1]
        return sides.astype(F32)

    def element(e, carry):
        @pl.when(e == jnp.where(g == 0, 3, 1))
        def _():
            pl.semaphore_wait(barrier, 3 * doms - 1)
            send_state()

        for copy in loads(e):
            copy.wait()
        coupled = dot_nt(inv_v[e], lt_v[e]).astype(BF16)
        removed = dot_nn(tl_v[e], coupled)
        edge = width // LANES * LANES
        schur_v[e, :, edge:wide] = (-removed[:, edge:wide]).astype(BF16)
        schur_v[e, :, 0:width] = (tt_v[e].astype(F32) - removed[:, 0:width]).astype(BF16)
        return carry

    lax.fori_loop(0, elements, element, 0)

    for copy in down_copies(True):
        copy.wait_recv()
    got = down_dst[...].astype(F32).reshape(table, LANES).astype(BF16)
    sides = dot_nn(fetch_hot, got)
    lane_side = iota((side_rows, LANES), 1)
    target = base + sides[:, fd : fd + 1]
    faces_in = spread_faces(jnp.where(lane_side < fd, sides, 0.0))
    vector = jnp.where(iota((ROWS, wide), 1) == width, -1.0, faces_in)
    trhs = jnp.concatenate(
        [trhs_ref[...].astype(F32), jnp.zeros((ROWS - elements, width), F32)], axis=0
    )
    mine = send_terms(0, apply(vector) - trhs)

    rows_own = 2 * doms * face_rows
    rows_all = 2 * rows_own
    for copy in term_copies(0, True):
        copy.wait_recv()
    first = term_dst[0].reshape(rows_all, LANES)
    lane_k = iota((ROWS, LANES), 1)
    weights = jnp.where(lane_k == fd, float(span), jnp.where(lane_k == fd + 1, 1.0, 0.0))
    keys = dot_nt(weights.astype(BF16), first)[0:1, :]
    keys = keys + jnp.where(iota((1, rows_all), 1) >= rows_own, 2.0 * doms * span, 0.0)
    partner = dot_nn(jnp.where(keys == target, 1.0, 0.0).astype(BF16), first)
    total = jnp.where(lane_side < fd, mine + partner, 0.0)
    send_terms(1, apply(spread_faces(total)))

    own_keys = keys[:, :rows_own]
    ask = [jnp.where(col < 0, -1, d * span + 1 + col).astype(F32) for col in face_cols]
    pick = (
        jnp.where(own_keys == ask[0], 1.0, 0.0) + jnp.where(own_keys == ask[1], 1.0, 0.0)
    ).astype(BF16)
    out_ref[0] = dot_nn(pick, first[:rows_own])
    for copy in down_copies() + term_copies(0):
        copy.wait_send()
    for copy in term_copies(1, True):
        copy.wait_recv()
    out_ref[1] = dot_nn(pick, term_dst[1, 0:2].reshape(rows_own, LANES))
    for copy in term_copies(1):
        copy.wait_send()


def on_device(grps, doms, *args):
    inv, lt, tl, tt, lrhs, trhs, state, owner, slot, faces = args
    elements, interior = inv.shape[0], inv.shape[1]
    width = tt.shape[1]
    wide = (width // LANES + 1) * LANES
    lt = jnp.swapaxes(lt, 1, 2)
    n_faces, fd = state.shape
    face_rows = (n_faces + 15) // 16 * 16
    vmem = pl.BlockSpec(memory_space=pltpu.VMEM)
    anys = pl.BlockSpec(memory_space=pl.ANY)
    out = pl.pallas_call(
        functools.partial(kernel, grps, doms),
        out_shape=jax.ShapeDtypeStruct((2, face_rows, LANES), F32),
        in_specs=[anys] * 10,
        out_specs=vmem,
        scratch_shapes=[
            pltpu.VMEM(lrhs.shape, BF16),
            pltpu.VMEM(trhs.shape, BF16),
            pltpu.VMEM(state.shape, BF16),
            pltpu.SMEM(owner.shape, jnp.int32),
            pltpu.SMEM(slot.shape, jnp.int32),
            pltpu.SMEM((2, n_faces), jnp.int32),
            pltpu.VMEM(inv.shape, BF16),
            pltpu.VMEM((elements, wide, interior), BF16),
            pltpu.VMEM(tl.shape, BF16),
            pltpu.VMEM(tt.shape, BF16),
            pltpu.VMEM((elements, width, wide), BF16),
            pltpu.VMEM((face_rows, LANES), F32),
            pltpu.VMEM((doms, ROWS, LANES), LINK),
            pltpu.VMEM((2, doms, ROWS, LANES), LINK),
            pltpu.VMEM((2, 2, face_rows, LANES), BF16),
            pltpu.VMEM((2, 4, doms, face_rows, LANES), BF16),
            pltpu.SemaphoreType.DMA((elements, 4)),
            pltpu.SemaphoreType.DMA((6,)),
            pltpu.SemaphoreType.DMA((2, doms)),
            pltpu.SemaphoreType.DMA((2, doms)),
            pltpu.SemaphoreType.DMA((2, 4, doms)),
            pltpu.SemaphoreType.DMA((2, 4, doms)),
        ],
        compiler_params=pltpu.CompilerParams(
            collective_id=0, has_side_effects=True, vmem_limit_bytes=24 * 1024 * 1024
        ),
    )(*[pltpu.with_memory_space_constraint(v, pltpu.HBM) for v in (inv, lt, tl, tt, lrhs, trhs, state, owner, slot, faces.T)])
    return out[0, :n_faces, :fd], out[1, :n_faces, :fd]


def solution(mesh):
    lead = ("grp", "dom")
    specs = (P(lead, None, None),) * 4 + (P(lead, None),) * 6
    return jax.shard_map(
        functools.partial(on_device, mesh.shape["grp"], mesh.shape["dom"]),
        mesh=mesh,
        in_specs=specs,
        out_specs=(P(lead, None), P(lead, None)),
        check_vma=False,
    )
```

```python
import functools

import jax
import jax.numpy as jnp
from jax import lax
from jax.experimental import pallas as pl
from jax.experimental.pallas import tpu as pltpu
from jax.sharding import PartitionSpec as P

F32 = jnp.float32
BF16 = jnp.bfloat16
LANES = 128
ROWS = 8
LINK = jnp.bfloat16
MESH = pl.DeviceIdType.MESH


def iota(shape, axis):
    return lax.broadcasted_iota(jnp.int32, shape, axis)


def dot_nn(a, b):
    return jnp.dot(a, b, preferred_element_type=F32)


def dot_nt(a, b):
    return lax.dot_general(a, b, (((1,), (1,)), ((), ())), preferred_element_type=F32)


def kernel(
    grps,
    doms,
    inv_hbm,
    lt_hbm,
    tl_hbm,
    tt_hbm,
    lrhs_hbm,
    trhs_hbm,
    state_hbm,
    owner_hbm,
    slot_hbm,
    face_hbm,
    out_ref,
    lrhs_ref,
    trhs_ref,
    state_ref,
    owner_ref,
    slot_ref,
    face_ref,
    inv_v,
    lt_v,
    tl_v,
    tt_v,
    schur_v,
    state_v,
    down_src,
    down_dst,
    term_src,
    term_dst,
    load_sem,
    small_sem,
    down_send,
    down_recv,
    term_send,
    term_recv,
):
    g = lax.axis_index("grp")
    d = lax.axis_index("dom")
    elements = inv_hbm.shape[0]
    width = tt_hbm.shape[1]
    faces = face_ref.shape[1]
    fd = state_ref.shape[1]
    per_elem = owner_ref.shape[1]
    cap = 2 * ((faces + doms - 1) // doms)
    span = doms * cap
    positions = doms * ROWS
    table = 2 * positions
    face_rows = state_v.shape[0]
    wide = (width // LANES + 1) * LANES
    up_g = lax.rem(g + 1, grps)
    dn_g = lax.rem(g + grps - 1, grps)

    def loads(e):
        pairs = (
            (inv_hbm, inv_v.at[e]),
            (lt_hbm, lt_v.at[e, pl.ds(0, width)]),
            (tl_hbm, tl_v.at[e]),
            (tt_hbm, tt_v.at[e]),
        )
        return [
            pltpu.make_async_copy(src.at[e], dst, load_sem.at[e, i])
            for i, (src, dst) in enumerate(pairs)
        ]

    smalls = [
        pltpu.make_async_copy(src, dst, small_sem.at[i])
        for i, (src, dst) in enumerate(
            (
                (owner_hbm, owner_ref),
                (slot_hbm, slot_ref),
                (face_hbm, face_ref),
                (state_hbm, state_ref),
                (lrhs_hbm, lrhs_ref),
                (trhs_hbm, trhs_ref),
            )
        )
    ]
    for copy in smalls:
        copy.start()

    barrier = pltpu.get_barrier_semaphore()
    for j in range(doms):
        peer = lax.rem(d + j, doms)
        for row in (up_g, dn_g) if j == 0 else (g, up_g, dn_g):
            pl.semaphore_signal(barrier, inc=1, device_id=(row, peer), device_id_type=MESH)

    for e in range(elements):
        for copy in loads(e):
            copy.start()

    for copy in smalls:
        copy.wait()

    def padded(pos):
        return pos // cap * ROWS + lax.rem(pos, cap)

    raw = [[face_ref[i, f] for f in range(faces)] for i in range(2)]
    lane8 = iota((ROWS, LANES), 1)
    row1 = iota((ROWS, 1), 0)
    face_iota = iota((face_rows, 1), 0)
    pos_iota = iota((positions, LANES), 0)
    hits, face_cols = [], []
    for i in range(2):
        row = jnp.full((ROWS, LANES), -1, jnp.int32)
        col = jnp.full((face_rows, 1), -1, jnp.int32)
        for f in range(faces):
            row = jnp.where(lane8 == f, padded(raw[i][f]), row)
            col = jnp.where(face_iota == f, raw[i][f], col)
        hits.append(jnp.where(pos_iota == row[0:1, :], 1.0, 0.0).astype(BF16)[:, :face_rows])
        face_cols.append(col)

    srow = jnp.full((ROWS, LANES), -1, jnp.int32)
    fetch_cols, base_cols, dom_cols, pos_cols = [], [], [], []
    low = jnp.int32(0)
    high = jnp.int32(0)
    for k in range(per_elem):
        fetch_col = jnp.full((ROWS, 1), -1, jnp.int32)
        base_col = jnp.full((ROWS, 1), -4 * doms * span, jnp.int32)
        dom_col = jnp.zeros((ROWS, 1), jnp.int32)
        pos_col = jnp.zeros((ROWS, 1), jnp.int32)
        for e in range(elements):
            owner = owner_ref[e, k]
            own_g = owner // doms
            own_d = owner - own_g * doms
            slot = slot_ref[e, k]
            lift = jnp.where(own_g == g, 0, 1)
            hit = row1 == e
            fetch_col = jnp.where(hit, lift * positions + own_d * ROWS + slot, fetch_col)
            base_col = jnp.where(hit, (2 * lift * doms + own_d) * span + 1, base_col)
            dom_col = jnp.where(hit, own_d, dom_col)
            pos_col = jnp.where(hit, d * cap + slot + 1, pos_col)
            place = jnp.where(own_g == g, low, face_rows + high)
            srow = jnp.where(lane8 == k * ROWS + e, place, srow)
            high = high + lift
            low = low + 1 - lift
        fetch_cols.append(fetch_col)
        base_cols.append(base_col)
        dom_cols.append(dom_col)
        pos_cols.append(pos_col)
    side_rows = per_elem * ROWS
    fetch_hot = jnp.where(
        iota((side_rows, table), 1) == jnp.concatenate(fetch_cols, axis=0), 1.0, 0.0
    ).astype(BF16)
    place_hot = jnp.where(iota((2 * face_rows, LANES), 0) == srow[0:1, :], 1.0, 0.0).astype(BF16)[
        :, :side_rows
    ]
    base = jnp.concatenate(base_cols, axis=0).astype(F32)
    lane_s = iota((side_rows, LANES), 1)
    stamp = jnp.where(
        lane_s == fd,
        jnp.concatenate(dom_cols, axis=0).astype(F32),
        jnp.where(lane_s == fd + 1, jnp.concatenate(pos_cols, axis=0).astype(F32), 0.0),
    ).astype(BF16)

    state_v[...] = jnp.zeros_like(state_v)
    state_v[0:faces, 0:fd] = state_ref[...].astype(F32)
    spare = wide - width
    rhs = lrhs_ref[...].astype(F32)
    spare_row = iota((spare, rhs.shape[1]), 0)
    for e in range(elements):
        lt_v[e, width:wide, :] = jnp.where(spare_row == 0, rhs[e : e + 1, :], 0.0).astype(BF16)

    def down_copies(incoming=False):
        copies = []
        for j in range(doms):
            peer = lax.rem(d + j, doms)
            for lift, row in ((0, g), (1, dn_g)):
                if j == 0 and lift == 0:
                    continue
                copies.append(
                    pltpu.make_async_remote_copy(
                        src_ref=down_src.at[peer],
                        dst_ref=down_dst.at[lift, peer if incoming else d],
                        send_sem=down_send.at[lift, peer],
                        recv_sem=down_recv.at[lift, peer if incoming else d],
                        device_id=(row, peer),
                        device_id_type=MESH,
                    )
                )
        return copies

    regions = ((0, g), (1, up_g), (0, dn_g), (1, g))

    def term_copies(turn, incoming=False):
        copies = []
        for j in range(doms):
            peer = lax.rem(d + j, doms)
            for r in range(4 - 2 * turn):
                half, row = regions[r]
                if j == 0 and r in (0, 3):
                    continue
                copies.append(
                    pltpu.make_async_remote_copy(
                        src_ref=term_src.at[turn, half],
                        dst_ref=term_dst.at[turn, r, peer if incoming else d],
                        send_sem=term_send.at[turn, r, peer],
                        recv_sem=term_recv.at[turn, r, peer if incoming else d],
                        device_id=(row, peer),
                        device_id_type=MESH,
                    )
                )
        return copies

    def send_state():
        lane_f = iota((face_rows, LANES), 1)
        rows = dot_nn(hits[0] + hits[1], state_v[...].astype(BF16))
        for i in range(2):
            other = jnp.where(lane_f == fd, face_cols[1 - i].astype(F32), 0.0).astype(BF16)
            rows = rows + dot_nn(hits[i], other)
        down_src[...] = rows.reshape(doms, ROWS, LANES).astype(LINK)
        for copy in down_copies():
            copy.start()
        down_dst[0, d] = down_src[d]

    def spread_faces(sides):
        total = jnp.zeros((ROWS, wide), F32)
        for k in range(per_elem):
            piece = jnp.concatenate(
                [sides[k * ROWS : (k + 1) * ROWS, :], jnp.zeros((ROWS, wide - LANES), F32)], axis=1
            )
            total = total + (piece if k == 0 else pltpu.roll(piece, k * fd, 1))
        return total

    row_wide = iota((ROWS, width), 0)

    def apply(vector):
        total = jnp.zeros((ROWS, width), F32)
        for e in range(elements):
            total = total + jnp.where(row_wide == e, dot_nt(vector.astype(BF16), schur_v[e]), 0.0)
        return total

    lane_fd = iota((ROWS, LANES), 1) < fd

    def send_terms(turn, terms):
        full = jnp.concatenate([terms, jnp.zeros((ROWS, wide - width), F32)], axis=1)
        pieces = []
        for k in range(per_elem):
            moved = full if k == 0 else pltpu.roll(full, wide - k * fd, 1)
            pieces.append(jnp.where(lane_fd, moved[:, :LANES], 0.0))
        sides = jnp.concatenate(pieces, axis=0).astype(BF16)
        rows = dot_nn(place_hot, sides + stamp)
        term_src[turn] = rows.reshape(2, face_rows, LANES).astype(BF16)
        for copy in term_copies(turn):
            copy.start()
        term_dst[turn, 0, d] = term_src[turn, 0]
        if turn == 0:
            term_dst[turn, 3, d] = term_src[turn, 1]
        return sides.astype(F32)

    def element(e, carry):
        @pl.when(e == jnp.where(g == 0, jnp.where(d < 2, 3, 2), 1))
        def _():
            pl.semaphore_wait(barrier, 3 * doms - 1)
            send_state()

        for copy in loads(e):
            copy.wait()
        coupled = dot_nt(inv_v[e], lt_v[e]).astype(BF16)
        removed = dot_nn(tl_v[e], coupled)
        edge = width // LANES * LANES
        schur_v[e, :, edge:wide] = (-removed[:, edge:wide]).astype(BF16)
        schur_v[e, :, 0:width] = (tt_v[e].astype(F32) - removed[:, 0:width]).astype(BF16)
        return carry

    lax.fori_loop(0, elements, element, 0)

    for copy in down_copies(True):
        copy.wait_recv()
    got = down_dst[...].astype(F32).reshape(table, LANES).astype(BF16)
    sides = dot_nn(fetch_hot, got)
    lane_side = iota((side_rows, LANES), 1)
    target = base + sides[:, fd : fd + 1]
    faces_in = spread_faces(jnp.where(lane_side < fd, sides, 0.0))
    vector = jnp.where(iota((ROWS, wide), 1) == width, -1.0, faces_in)
    trhs = jnp.concatenate(
        [trhs_ref[...].astype(F32), jnp.zeros((ROWS - elements, width), F32)], axis=0
    )
    mine = send_terms(0, apply(vector) - trhs)

    rows_own = 2 * doms * face_rows
    rows_all = 2 * rows_own
    for copy in term_copies(0, True):
        copy.wait_recv()
    first = term_dst[0].reshape(rows_all, LANES)
    lane_k = iota((ROWS, LANES), 1)
    weights = jnp.where(lane_k == fd, float(span), jnp.where(lane_k == fd + 1, 1.0, 0.0))
    keys = dot_nt(weights.astype(BF16), first)[0:1, :]
    keys = keys + jnp.where(iota((1, rows_all), 1) >= rows_own, 2.0 * doms * span, 0.0)
    partner = dot_nn(jnp.where(keys == target, 1.0, 0.0).astype(BF16), first)
    total = jnp.where(lane_side < fd, mine + partner, 0.0)
    send_terms(1, apply(spread_faces(total)))

    own_keys = keys[:, :rows_own]
    ask = [jnp.where(col < 0, -1, d * span + 1 + col).astype(F32) for col in face_cols]
    pick = (
        jnp.where(own_keys == ask[0], 1.0, 0.0) + jnp.where(own_keys == ask[1], 1.0, 0.0)
    ).astype(BF16)
    out_ref[0] = dot_nn(pick, first[:rows_own])
    for copy in down_copies() + term_copies(0):
        copy.wait_send()
    for copy in term_copies(1, True):
        copy.wait_recv()
    out_ref[1] = dot_nn(pick, term_dst[1, 0:2].reshape(rows_own, LANES))
    for copy in term_copies(1):
        copy.wait_send()


def on_device(grps, doms, *args):
    inv, lt, tl, tt, lrhs, trhs, state, owner, slot, faces = args
    elements, interior = inv.shape[0], inv.shape[1]
    width = tt.shape[1]
    wide = (width // LANES + 1) * LANES
    lt = jnp.swapaxes(lt, 1, 2)
    n_faces, fd = state.shape
    face_rows = (n_faces + 15) // 16 * 16
    vmem = pl.BlockSpec(memory_space=pltpu.VMEM)
    anys = pl.BlockSpec(memory_space=pl.ANY)
    out = pl.pallas_call(
        functools.partial(kernel, grps, doms),
        out_shape=jax.ShapeDtypeStruct((2, face_rows, LANES), F32),
        in_specs=[anys] * 10,
        out_specs=vmem,
        scratch_shapes=[
            pltpu.VMEM(lrhs.shape, BF16),
            pltpu.VMEM(trhs.shape, BF16),
            pltpu.VMEM(state.shape, BF16),
            pltpu.SMEM(owner.shape, jnp.int32),
            pltpu.SMEM(slot.shape, jnp.int32),
            pltpu.SMEM((2, n_faces), jnp.int32),
            pltpu.VMEM(inv.shape, BF16),
            pltpu.VMEM((elements, wide, interior), BF16),
            pltpu.VMEM(tl.shape, BF16),
            pltpu.VMEM(tt.shape, BF16),
            pltpu.VMEM((elements, width, wide), BF16),
            pltpu.VMEM((face_rows, LANES), F32),
            pltpu.VMEM((doms, ROWS, LANES), LINK),
            pltpu.VMEM((2, doms, ROWS, LANES), LINK),
            pltpu.VMEM((2, 2, face_rows, LANES), BF16),
            pltpu.VMEM((2, 4, doms, face_rows, LANES), BF16),
            pltpu.SemaphoreType.DMA((elements, 4)),
            pltpu.SemaphoreType.DMA((6,)),
            pltpu.SemaphoreType.DMA((2, doms)),
            pltpu.SemaphoreType.DMA((2, doms)),
            pltpu.SemaphoreType.DMA((2, 4, doms)),
            pltpu.SemaphoreType.DMA((2, 4, doms)),
        ],
        compiler_params=pltpu.CompilerParams(
            collective_id=0, has_side_effects=True, vmem_limit_bytes=24 * 1024 * 1024
        ),
    )(*[pltpu.with_memory_space_constraint(v, pltpu.HBM) for v in (inv, lt, tl, tt, lrhs, trhs, state, owner, slot, faces.T)])
    return out[0, :n_faces, :fd], out[1, :n_faces, :fd]


def solution(mesh):
    lead = ("grp", "dom")
    specs = (P(lead, None, None),) * 4 + (P(lead, None),) * 6
    return jax.shard_map(
        functools.partial(on_device, mesh.shape["grp"], mesh.shape["dom"]),
        mesh=mesh,
        in_specs=specs,
        out_specs=(P(lead, None), P(lead, None)),
        check_vma=False,
    )
```

```python
import functools

import jax
import jax.numpy as jnp
from jax import lax
from jax.experimental import pallas as pl
from jax.experimental.pallas import tpu as pltpu
from jax.sharding import PartitionSpec as P

F32 = jnp.float32
BF16 = jnp.bfloat16
LANES = 128
ROWS = 8
LINK = jnp.bfloat16
MESH = pl.DeviceIdType.MESH


def iota(shape, axis):
    return lax.broadcasted_iota(jnp.int32, shape, axis)


def dot_nn(a, b):
    return jnp.dot(a, b, preferred_element_type=F32)


def dot_nt(a, b):
    return lax.dot_general(a, b, (((1,), (1,)), ((), ())), preferred_element_type=F32)


def kernel(
    grps,
    doms,
    inv_hbm,
    lt_hbm,
    tl_hbm,
    tt_hbm,
    lrhs_hbm,
    trhs_hbm,
    state_hbm,
    owner_hbm,
    slot_hbm,
    face_hbm,
    out_ref,
    lrhs_ref,
    trhs_ref,
    state_ref,
    owner_ref,
    slot_ref,
    face_ref,
    inv_v,
    lt_v,
    tl_v,
    tt_v,
    schur_v,
    state_v,
    down_src,
    down_dst,
    term_src,
    term_dst,
    load_sem,
    small_sem,
    down_send,
    down_recv,
    term_send,
    term_recv,
):
    g = lax.axis_index("grp")
    d = lax.axis_index("dom")
    elements = inv_hbm.shape[0]
    width = tt_hbm.shape[1]
    faces = face_ref.shape[1]
    fd = state_ref.shape[1]
    per_elem = owner_ref.shape[1]
    cap = 2 * ((faces + doms - 1) // doms)
    span = doms * cap
    positions = doms * ROWS
    table = 2 * positions
    face_rows = state_v.shape[0]
    wide = (width // LANES + 1) * LANES
    up_g = lax.rem(g + 1, grps)
    dn_g = lax.rem(g + grps - 1, grps)

    def loads(e):
        pairs = (
            (inv_hbm, inv_v.at[e]),
            (lt_hbm, lt_v.at[e, pl.ds(0, width)]),
            (tl_hbm, tl_v.at[e]),
            (tt_hbm, tt_v.at[e]),
        )
        return [
            pltpu.make_async_copy(src.at[e], dst, load_sem.at[e, i])
            for i, (src, dst) in enumerate(pairs)
        ]

    smalls = [
        pltpu.make_async_copy(src, dst, small_sem.at[i])
        for i, (src, dst) in enumerate(
            (
                (owner_hbm, owner_ref),
                (slot_hbm, slot_ref),
                (face_hbm, face_ref),
                (state_hbm, state_ref),
                (lrhs_hbm, lrhs_ref),
                (trhs_hbm, trhs_ref),
            )
        )
    ]
    for copy in smalls:
        copy.start()

    barrier = pltpu.get_barrier_semaphore()
    for row in (up_g, dn_g, g):
        for j in range(1 if row is g else 0, doms):
            peer = lax.rem(d + j, doms)
            pl.semaphore_signal(barrier, inc=1, device_id=(row, peer), device_id_type=MESH)

    for e in range(elements):
        for copy in loads(e):
            copy.start()

    for copy in smalls:
        copy.wait()

    def padded(pos):
        return pos // cap * ROWS + lax.rem(pos, cap)

    raw = [[face_ref[i, f] for f in range(faces)] for i in range(2)]
    lane8 = iota((ROWS, LANES), 1)
    row1 = iota((ROWS, 1), 0)
    face_iota = iota((face_rows, 1), 0)
    pos_iota = iota((positions, LANES), 0)
    hits, face_cols = [], []
    for i in range(2):
        row = jnp.full((ROWS, LANES), -1, jnp.int32)
        col = jnp.full((face_rows, 1), -1, jnp.int32)
        for f in range(faces):
            row = jnp.where(lane8 == f, padded(raw[i][f]), row)
            col = jnp.where(face_iota == f, raw[i][f], col)
        hits.append(jnp.where(pos_iota == row[0:1, :], 1.0, 0.0).astype(BF16)[:, :face_rows])
        face_cols.append(col)

    srow = jnp.full((ROWS, LANES), -1, jnp.int32)
    fetch_cols, base_cols, dom_cols, pos_cols = [], [], [], []
    low = jnp.int32(0)
    high = jnp.int32(0)
    for k in range(per_elem):
        fetch_col = jnp.full((ROWS, 1), -1, jnp.int32)
        base_col = jnp.full((ROWS, 1), -4 * doms * span, jnp.int32)
        dom_col = jnp.zeros((ROWS, 1), jnp.int32)
        pos_col = jnp.zeros((ROWS, 1), jnp.int32)
        for e in range(elements):
            owner = owner_ref[e, k]
            own_g = owner // doms
            own_d = owner - own_g * doms
            slot = slot_ref[e, k]
            lift = jnp.where(own_g == g, 0, 1)
            hit = row1 == e
            fetch_col = jnp.where(hit, lift * positions + own_d * ROWS + slot, fetch_col)
            base_col = jnp.where(hit, (2 * lift * doms + own_d) * span + 1, base_col)
            dom_col = jnp.where(hit, own_d, dom_col)
            pos_col = jnp.where(hit, d * cap + slot + 1, pos_col)
            place = jnp.where(own_g == g, low, face_rows + high)
            srow = jnp.where(lane8 == k * ROWS + e, place, srow)
            high = high + lift
            low = low + 1 - lift
        fetch_cols.append(fetch_col)
        base_cols.append(base_col)
        dom_cols.append(dom_col)
        pos_cols.append(pos_col)
    side_rows = per_elem * ROWS
    fetch_hot = jnp.where(
        iota((side_rows, table), 1) == jnp.concatenate(fetch_cols, axis=0), 1.0, 0.0
    ).astype(BF16)
    place_hot = jnp.where(iota((2 * face_rows, LANES), 0) == srow[0:1, :], 1.0, 0.0).astype(BF16)[
        :, :side_rows
    ]
    base = jnp.concatenate(base_cols, axis=0).astype(F32)
    lane_s = iota((side_rows, LANES), 1)
    stamp = jnp.where(
        lane_s == fd,
        jnp.concatenate(dom_cols, axis=0).astype(F32),
        jnp.where(lane_s == fd + 1, jnp.concatenate(pos_cols, axis=0).astype(F32), 0.0),
    ).astype(BF16)

    state_v[...] = jnp.zeros_like(state_v)
    state_v[0:faces, 0:fd] = state_ref[...].astype(F32)
    spare = wide - width
    rhs = lrhs_ref[...].astype(F32)
    spare_row = iota((spare, rhs.shape[1]), 0)
    for e in range(elements):
        lt_v[e, width:wide, :] = jnp.where(spare_row == 0, rhs[e : e + 1, :], 0.0).astype(BF16)

    def down_copies(incoming=False):
        copies = []
        for j in range(doms):
            peer = lax.rem(d + j, doms)
            for lift, row in ((0, g), (1, dn_g)):
                if j == 0 and lift == 0:
                    continue
                copies.append(
                    pltpu.make_async_remote_copy(
                        src_ref=down_src.at[peer],
                        dst_ref=down_dst.at[lift, peer if incoming else d],
                        send_sem=down_send.at[lift, peer],
                        recv_sem=down_recv.at[0],
                        device_id=(row, peer),
                        device_id_type=MESH,
                    )
                )
        return copies

    regions = ((0, g), (1, up_g), (0, dn_g), (1, g))

    def term_copies(turn, incoming=False):
        copies = []
        for j in range(doms):
            peer = lax.rem(d + j, doms)
            for r in range(4 - 2 * turn):
                half, row = regions[r]
                if j == 0 and r in (0, 3):
                    continue
                copies.append(
                    pltpu.make_async_remote_copy(
                        src_ref=term_src.at[turn, half],
                        dst_ref=term_dst.at[turn, r, peer if incoming else d],
                        send_sem=term_send.at[turn, r, peer],
                        recv_sem=term_recv.at[turn],
                        device_id=(row, peer),
                        device_id_type=MESH,
                    )
                )
        return copies

    def send_state():
        lane_f = iota((face_rows, LANES), 1)
        rows = dot_nn(hits[0] + hits[1], state_v[...].astype(BF16))
        for i in range(2):
            other = jnp.where(lane_f == fd, face_cols[1 - i].astype(F32), 0.0).astype(BF16)
            rows = rows + dot_nn(hits[i], other)
        down_src[...] = rows.reshape(doms, ROWS, LANES).astype(LINK)
        for copy in down_copies():
            copy.start()
        pltpu.make_async_copy(down_src.at[d], down_dst.at[0, d], down_recv.at[0]).start()

    def spread_faces(sides):
        total = jnp.zeros((ROWS, wide), F32)
        for k in range(per_elem):
            piece = jnp.concatenate(
                [sides[k * ROWS : (k + 1) * ROWS, :], jnp.zeros((ROWS, wide - LANES), F32)], axis=1
            )
            total = total + (piece if k == 0 else pltpu.roll(piece, k * fd, 1))
        return total

    row_wide = iota((ROWS, width), 0)

    def apply(vector):
        total = jnp.zeros((ROWS, width), F32)
        for e in range(elements):
            total = total + jnp.where(row_wide == e, dot_nt(vector.astype(BF16), schur_v[e]), 0.0)
        return total

    lane_fd = iota((ROWS, LANES), 1) < fd

    def send_terms(turn, terms):
        full = jnp.concatenate([terms, jnp.zeros((ROWS, wide - width), F32)], axis=1)
        pieces = []
        for k in range(per_elem):
            moved = full if k == 0 else pltpu.roll(full, wide - k * fd, 1)
            pieces.append(jnp.where(lane_fd, moved[:, :LANES], 0.0))
        sides = jnp.concatenate(pieces, axis=0).astype(BF16)
        rows = dot_nn(place_hot, sides + stamp)
        term_src[turn] = rows.reshape(2, face_rows, LANES).astype(BF16)
        for copy in term_copies(turn):
            copy.start()
        for r in (0, 3) if turn == 0 else (0,):
            pltpu.make_async_copy(
                term_src.at[turn, regions[r][0]], term_dst.at[turn, r, d], term_recv.at[turn]
            ).start()
        return sides.astype(F32)

    def element(e, carry):
        @pl.when(e == jnp.where(g == 0, jnp.where(d < 2, 3, 2), 1))
        def _():
            pl.semaphore_wait(barrier, 3 * doms - 1)
            send_state()

        for copy in loads(e):
            copy.wait()
        coupled = dot_nt(inv_v[e], lt_v[e]).astype(BF16)
        removed = dot_nn(tl_v[e], coupled)
        edge = width // LANES * LANES
        schur_v[e, :, edge:wide] = (-removed[:, edge:wide]).astype(BF16)
        schur_v[e, :, 0:width] = (tt_v[e].astype(F32) - removed[:, 0:width]).astype(BF16)
        return carry

    lax.fori_loop(0, elements, element, 0)

    pltpu.make_async_copy(down_dst, down_dst, down_recv.at[0]).wait()
    got = down_dst[...].astype(F32).reshape(table, LANES).astype(BF16)
    sides = dot_nn(fetch_hot, got)
    lane_side = iota((side_rows, LANES), 1)
    target = base + sides[:, fd : fd + 1]
    faces_in = spread_faces(jnp.where(lane_side < fd, sides, 0.0))
    vector = jnp.where(iota((ROWS, wide), 1) == width, -1.0, faces_in)
    trhs = jnp.concatenate(
        [trhs_ref[...].astype(F32), jnp.zeros((ROWS - elements, width), F32)], axis=0
    )
    mine = send_terms(0, apply(vector) - trhs)

    rows_own = 2 * doms * face_rows
    rows_all = 2 * rows_own
    pltpu.make_async_copy(term_dst.at[0], term_dst.at[0], term_recv.at[0]).wait()
    first = term_dst[0].reshape(rows_all, LANES)
    lane_k = iota((ROWS, LANES), 1)
    weights = jnp.where(lane_k == fd, float(span), jnp.where(lane_k == fd + 1, 1.0, 0.0))
    keys = dot_nt(weights.astype(BF16), first)[0:1, :]
    keys = keys + jnp.where(iota((1, rows_all), 1) >= rows_own, 2.0 * doms * span, 0.0)
    partner = dot_nn(jnp.where(keys == target, 1.0, 0.0).astype(BF16), first)
    total = jnp.where(lane_side < fd, mine + partner, 0.0)
    send_terms(1, apply(spread_faces(total)))

    own_keys = keys[:, :rows_own]
    ask = [jnp.where(col < 0, -1, d * span + 1 + col).astype(F32) for col in face_cols]
    pick = (
        jnp.where(own_keys == ask[0], 1.0, 0.0) + jnp.where(own_keys == ask[1], 1.0, 0.0)
    ).astype(BF16)
    out_ref[0] = dot_nn(pick, first[:rows_own])
    for copy in down_copies() + term_copies(0) + term_copies(1):
        copy.wait_send()
    pltpu.make_async_copy(term_dst.at[1, 0:2], term_dst.at[1, 0:2], term_recv.at[1]).wait()
    out_ref[1] = dot_nn(pick, term_dst[1, 0:2].reshape(rows_own, LANES))


def on_device(grps, doms, *args):
    inv, lt, tl, tt, lrhs, trhs, state, owner, slot, faces = args
    elements, interior = inv.shape[0], inv.shape[1]
    width = tt.shape[1]
    wide = (width // LANES + 1) * LANES
    lt = jnp.swapaxes(lt, 1, 2)
    n_faces, fd = state.shape
    face_rows = (n_faces + 15) // 16 * 16
    vmem = pl.BlockSpec(memory_space=pltpu.VMEM)
    anys = pl.BlockSpec(memory_space=pl.ANY)
    out = pl.pallas_call(
        functools.partial(kernel, grps, doms),
        out_shape=jax.ShapeDtypeStruct((2, face_rows, LANES), F32),
        in_specs=[anys] * 10,
        out_specs=vmem,
        scratch_shapes=[
            pltpu.VMEM(lrhs.shape, BF16),
            pltpu.VMEM(trhs.shape, BF16),
            pltpu.VMEM(state.shape, BF16),
            pltpu.SMEM(owner.shape, jnp.int32),
            pltpu.SMEM(slot.shape, jnp.int32),
            pltpu.SMEM((2, n_faces), jnp.int32),
            pltpu.VMEM(inv.shape, BF16),
            pltpu.VMEM((elements, wide, interior), BF16),
            pltpu.VMEM(tl.shape, BF16),
            pltpu.VMEM(tt.shape, BF16),
            pltpu.VMEM((elements, width, wide), BF16),
            pltpu.VMEM((face_rows, LANES), F32),
            pltpu.VMEM((doms, ROWS, LANES), LINK),
            pltpu.VMEM((2, doms, ROWS, LANES), LINK),
            pltpu.VMEM((2, 2, face_rows, LANES), BF16),
            pltpu.VMEM((2, 4, doms, face_rows, LANES), BF16),
            pltpu.SemaphoreType.DMA((elements, 4)),
            pltpu.SemaphoreType.DMA((6,)),
            pltpu.SemaphoreType.DMA((2, doms)),
            pltpu.SemaphoreType.DMA((1,)),
            pltpu.SemaphoreType.DMA((2, 4, doms)),
            pltpu.SemaphoreType.DMA((2,)),
        ],
        compiler_params=pltpu.CompilerParams(
            collective_id=0, has_side_effects=True, vmem_limit_bytes=24 * 1024 * 1024
        ),
    )(*[pltpu.with_memory_space_constraint(v, pltpu.HBM) for v in (inv, lt, tl, tt, lrhs, trhs, state, owner, slot, faces.T)])
    return out[0, :n_faces, :fd], out[1, :n_faces, :fd]


def solution(mesh):
    lead = ("grp", "dom")
    specs = (P(lead, None, None),) * 4 + (P(lead, None),) * 6
    return jax.shard_map(
        functools.partial(on_device, mesh.shape["grp"], mesh.shape["dom"]),
        mesh=mesh,
        in_specs=specs,
        out_specs=(P(lead, None), P(lead, None)),
        check_vma=False,
    )
```
